256 devices in a mesh: vocab: 16 (over z, core), feat: 16 (over y, x).
Axes of the slice: x: 4, y: 4, z: 8, core: 2. Of those that a mesh axis runs over, the one named last changes fastest.
Arguments:
- clean_hidden: bfloat16 [512, 3584], P(('vocab', 'feat')), may hold values from -6 to 6
- patched_hidden: bfloat16 [512, 3584], P(('vocab', 'feat')), may hold values from -6 to 6
- unembed: bfloat16 [3584, 131072], P(None, ('vocab', 'feat')), may hold values from -3.9 to 3.9, as said below
- norm_gain: float32 [3584], replicated, may hold values from 0.25 to 1.75
- enc_weight: bfloat16 [3584, 131072], P(None, ('vocab', 'feat')), may hold values from -0.09375 to 0.09375
- enc_bias: float32 [131072], P(('vocab', 'feat')), may hold values from -3 to 3
- threshold: float32 [131072], P(('vocab', 'feat')), may hold values from 0.1 to 1
- dec_weight: bfloat16 [131072, 3584], P(('vocab', 'feat')), may hold values from -0.09375 to 0.09375
- clean_next: int32 [512], replicated, may hold values from 0 to 131071
- patched_next: int32 [512], replicated, may hold values from 0 to 131071
- patch_pos: int32 [8], replicated, may hold values from 1 to 63
Outputs:
- attribution: float32 [8, 131072], P(None, ('vocab', 'feat'))
- metric: float32 [8], replicated
The draws below stay inside these ranges and needn't reach their ends.
Inputs may be any that keep to these rules, and one draw needn't show every extreme that they name: `unembed`: bounded entries.
All inputs are finite; a program needn't handle non-finite values.
Results may differ from the reference program's by a relative error of at most 0.0047.
Values may be sent and summed in bfloat16 or wider, within the bound.
A program may use at most 128 MiB of HBM per device.

```python
import math
import jax
import jax.numpy as jnp
import numpy as np
from jax import lax

D = 3584
VOCAB = 131072
FEATURES = 131072
SEQ = 64
PAIRS = 8
TOKENS = 512


def draw_unembed(key, part):
    key_values, key_scale = jax.random.split(key)
    column_pos = jnp.arange(VOCAB, dtype=jnp.float32) / VOCAB
    entries = jnp.clip(jax.random.normal(key_values, (D, VOCAB), jnp.float32), -4.0, 4.0)
    spread = jax.random.uniform(key_scale, (1, VOCAB), jnp.float32, 0.0, 1.0)
    scale_row = 0.02 * 10.0 ** spread * 3.0 ** column_pos[None, :]
    return (entries * scale_row).astype(jnp.bfloat16)


def plant(array, own_key, low, largest):
    index_at = [jax.random.randint(jax.random.fold_in(own_key, axis), (), 0, length) for axis, length in enumerate(array.shape)]
    main_axis = array.shape.index(max(array.shape))
    next_to = index_at[:main_axis] + [(index_at[main_axis] + 1) % array.shape[main_axis]] + index_at[main_axis + 1:]
    return array.at[tuple(index_at)].set(low).at[tuple(next_to)].set(largest)


def block_levels(key, dims, shards, least, largest):
    gain = 1.0
    for position, blocks in shards:
        heights = jax.random.uniform(jax.random.fold_in(jax.random.fold_in(key, 6), position), (blocks,), jnp.float32, least / len(shards), largest / len(shards))
        gain = gain * jnp.repeat(jnp.exp(heights), dims[position] // blocks).reshape((-1,) + (1,) * (len(dims) - 1 - position))
    return gain


def skewed_wide(stream_key, dims, amount, skew):
    portions = [min(1 << octave, amount + 1 - (1 << octave)) * (1 << 20) // math.isqrt((1 << octave) ** skew) + 1 for octave in range((amount + 1).bit_length()) if 1 << octave <= amount]
    width = 1 + sum(portions) // (1 << 30)
    listing = np.cumsum(np.array([max(1, weight // width) for weight in portions]))
    ticket = jax.random.randint(jax.random.fold_in(stream_key, 1), dims, 0, int(listing[len(portions) - 1]))
    start = jnp.left_shift(1, jnp.searchsorted(jnp.asarray(listing, jnp.int32), ticket, side="right").astype(jnp.int32))
    rank = start - 1 + jax.random.randint(jax.random.fold_in(stream_key, 4), dims, 0, 1 << 30) % jnp.minimum(start, amount + 1 - start)
    return jax.random.permutation(jax.random.fold_in(stream_key, 2), amount)[rank].astype(jnp.int32)


def centred(key, extent, scale, most, pieces=(), kind=jnp.bfloat16):
    result = scale * jax.random.normal(key, extent, jnp.float32)
    if pieces:
        result = result * block_levels(key, extent, pieces, -0.22, 0.18)
    return jnp.clip(result, -most, most).astype(kind)


def setup_inputs(seed: int = 0) -> dict:
    streams_of = jax.random.split(jax.random.key(seed), 12)
    clean_hidden = centred(streams_of[0], (TOKENS, D), 1.0, 6.0, ((0, 256),))
    patched_hidden = centred(streams_of[1], (TOKENS, D), 1.0, 6.0, ((0, 256),))
    unembed = draw_unembed(jax.random.fold_in(streams_of[11], 71), 0)
    norm_gain = jnp.clip(1.0 + 0.15 * jax.random.normal(streams_of[3], (D,), jnp.float32), 0.25, 1.75)
    enc_weight = centred(streams_of[4], (D, FEATURES), D ** -0.5, 0.09375, ((1, 256),))
    enc_bias = centred(streams_of[5], (FEATURES,), 0.5, 3.0, ((0, 256),), jnp.float32)
    threshold = jnp.clip(jnp.exp(math.log(1.0) - 2.3025851 * jax.random.uniform(streams_of[6], (FEATURES,), jnp.float32) ** block_levels(streams_of[6], (FEATURES,), ((0, 256),), -0.2, 0.2)), 0.1, 1.0)
    dec_weight = centred(streams_of[7], (FEATURES, D), D ** -0.5, 0.09375, ((0, 256),))
    clean_next = plant(skewed_wide(streams_of[8], (TOKENS,), VOCAB, 2), jax.random.fold_in(streams_of[8], 3), 0, VOCAB - 1).astype(jnp.int32)
    patched_next = plant(skewed_wide(streams_of[9], (TOKENS,), VOCAB, 2), jax.random.fold_in(streams_of[9], 3), 0, VOCAB - 1).astype(jnp.int32)
    patch_pos = plant(jax.random.randint(streams_of[10], (PAIRS,), 1, SEQ), jax.random.fold_in(streams_of[10], 1), 1, SEQ - 1).astype(jnp.int32)
    return dict(clean_hidden=clean_hidden, patched_hidden=patched_hidden, unembed=unembed, norm_gain=norm_gain, enc_weight=enc_weight, enc_bias=enc_bias, threshold=threshold, dec_weight=dec_weight, clean_next=clean_next, patched_next=patched_next, patch_pos=patch_pos)


logit_cap = 30.0
norm_eps = 1e-06
contract_last = (((1,), (1,)), ((), ()))

def normalize(hidden, norm_gain):
    values = hidden.astype(jnp.float32)
    inverse = lax.rsqrt(lax.optimization_barrier(jnp.mean(values * values, axis=1, keepdims=True)) + norm_eps)
    return ((values * inverse * norm_gain[None, :]).astype(jnp.bfloat16), values, inverse)

def capped(normed, unembed):
    raw_logit = jnp.dot(normed, unembed, preferred_element_type=jnp.float32)
    return logit_cap * jnp.tanh(raw_logit / logit_cap)

def reference(clean_hidden, patched_hidden, unembed, norm_gain, enc_weight, enc_bias, threshold, dec_weight, clean_next, patched_next, patch_pos):
    norm_clean, values_clean, inverse_clean = normalize(clean_hidden, norm_gain)
    norm_patched, values_patched, inverse_patched = normalize(patched_hidden, norm_gain)
    logit_clean = capped(norm_clean, unembed)
    logit_patched = capped(norm_patched, unembed)
    exp_clean = jnp.exp(logit_clean - logit_cap)
    exp_patched = jnp.exp(logit_patched - logit_cap)
    total_clean = lax.optimization_barrier(jnp.sum(exp_clean, 1))
    total_patched = lax.optimization_barrier(jnp.sum(exp_patched, 1))
    cross_sum = lax.optimization_barrier(jnp.sum(exp_clean * (logit_clean - logit_patched), 1))
    vocab_ids = lax.broadcasted_iota(jnp.int32, (1, VOCAB), 1)
    target = (clean_next[:, None] == vocab_ids).astype(jnp.float32) - (patched_next[:, None] == vocab_ids).astype(jnp.float32)
    picked = lax.optimization_barrier(jnp.sum(target * logit_patched, 1))
    token_ids = jnp.arange(TOKENS, dtype=jnp.int32)
    pair_hot = (token_ids // SEQ)[:, None] == jnp.arange(PAIRS, dtype=jnp.int32)[None, :]
    start_pos = lax.optimization_barrier(jnp.sum(jnp.where(pair_hot, patch_pos[None, :], 0), 1))
    active = (token_ids % SEQ >= start_pos).astype(jnp.float32)
    per_token = active * (cross_sum / total_clean - jnp.log(total_clean) + jnp.log(total_patched) + picked)
    metric = lax.optimization_barrier(jnp.sum(jnp.where(pair_hot, per_token[:, None], 0.0), 0))
    slope_term = 1.0 - (logit_patched / logit_cap) ** 2
    dlogit = (active[:, None] * (exp_patched / total_patched[:, None] - exp_clean / total_clean[:, None] + target) * slope_term).astype(jnp.bfloat16)
    dnormed = lax.dot_general(dlogit, unembed, contract_last, preferred_element_type=jnp.float32)
    weighted = dnormed * norm_gain[None, :]
    inner_sum = lax.optimization_barrier(jnp.sum(weighted * values_patched, 1, keepdims=True))
    grad_hidden = (inverse_patched * weighted - inverse_patched ** 3 * values_patched * inner_sum / D).astype(jnp.bfloat16)
    act_clean = jnp.maximum(jnp.dot(clean_hidden, enc_weight, preferred_element_type=jnp.float32) + enc_bias[None, :] - threshold[None, :], 0.0)
    act_patched = jnp.maximum(jnp.dot(patched_hidden, enc_weight, preferred_element_type=jnp.float32) + enc_bias[None, :] - threshold[None, :], 0.0)
    project = lax.dot_general(grad_hidden, dec_weight, contract_last, preferred_element_type=jnp.float32)
    attribution = lax.optimization_barrier(jnp.sum(((act_patched - act_clean) * project).reshape(PAIRS, SEQ, FEATURES), 1))
    return (attribution, metric)
```

```python
import jax
import jax.numpy as jnp
from jax import lax
from jax.experimental import pallas as pl
from jax.experimental.pallas import tpu as pltpu
from jax.sharding import PartitionSpec as P

SEQ = 64
CAP = 30.0
EPS = 1e-06
MESH = pl.DeviceIdType.MESH
NT = (((1,), (1,)), ((), ()))
D = 3584
PART = D // 2
QUART = D // 4
VL = 512
TN = 256
NCOPY = 160
F32 = jnp.float32
BF16 = jnp.bfloat16


def kernel(
    clean_ref, patched_ref, w_ref, e_ref, d_ref, gain_ref, bt_ref, meta_ref,
    attr_ref, metric_ref,
    wv, ev, dv, zbuf, fbuf, xb, nb, lpb, ecb, epb, difb, dlb, pb, r1w, r2w, qb, r1u, r2u,
    tb, zr, vb, gb, sx, sy, sz, acc, fin, finr, met, metr, btv, btr,
    send, recv, loc,
):
    v = lax.axis_index("vocab")
    f = lax.axis_index("feat")
    z, c = v // 2, v % 2
    y, x = f // 4, f % 4

    def at_x(o):
        return (v, y * 4 + (x + o) % 4)

    def at_y(o):
        return (v, ((y + o) % 4) * 4 + x)

    def at_z(o):
        return (((z + o) % 8) * 2 + c, f)

    sib = (z * 2 + (1 - c), f)
    ids = iter(range(NCOPY))
    sent = []

    def rcopy(src, dst, dev):
        k = next(ids)
        d = pltpu.make_async_remote_copy(
            src_ref=src, dst_ref=dst, send_sem=send.at[k], recv_sem=recv.at[k],
            device_id=dev, device_id_type=MESH,
        )
        d.start()
        sent.append(d)
        return d

    hl = [
        pltpu.make_async_copy(clean_ref, zbuf.at[z, 0], loc.at[0]),
        pltpu.make_async_copy(patched_ref, zbuf.at[z, 1], loc.at[1]),
    ]
    wl = [
        pltpu.make_async_copy(w_ref, wv.at[c], loc.at[2]),
        pltpu.make_async_copy(e_ref, ev.at[c], loc.at[3]),
        pltpu.make_async_copy(d_ref, dv.at[c], loc.at[4]),
        pltpu.make_async_copy(bt_ref, btv.at[c], loc.at[5]),
    ]
    for d in hl + wl:
        d.start()

    bar = pltpu.get_barrier_semaphore()
    partners = [at_x(o) for o in (1, 2, 3)] + [at_y(o) for o in (1, 2, 3)]
    partners += [at_z(o) for o in range(1, 8)] + [sib]
    for dev in partners:
        pl.semaphore_signal(bar, inc=1, device_id=dev, device_id_type=MESH)
    pl.semaphore_wait(bar, len(partners))

    for d in hl:
        d.wait()
    zc = [rcopy(zbuf.at[z], zbuf.at[z], at_z(o)) for o in (4, 3, 5, 2, 6, 1, 7)]
    wc = [
        rcopy(w_ref, wv.at[c], sib),
        rcopy(e_ref, ev.at[c], sib),
        rcopy(d_ref, dv.at[c], sib),
        rcopy(bt_ref, btv.at[c], sib),
    ]
    for d in zc:
        d.wait_recv()
    for zz in range(8):
        for run in range(2):
            fbuf[run, 2 * zz : 2 * zz + 2, :] = zbuf[zz, run].astype(F32)
    own = pl.multiple_of((x * 4 + y) * 16, 16)
    for run in range(2):
        xb[run, pl.ds(own, 16), :] = fbuf[run].astype(BF16)

    def gather_xy(buf):
        def row(part, cu, cw):
            b = cw * 4 + cu if part == 0 else cu * 4 + cw
            return pl.multiple_of(b * 16, 16)

        def blk(part, cu, cw, half=None):
            if half is None:
                cols = pl.ds(part * PART, PART)
            else:
                cols = pl.ds(part * PART + half * QUART, QUART)
            return buf.at[:, pl.ds(row(part, cu, cw), 16), cols]

        pos = ((y, x), (x, y))
        to_u = (at_y, at_x)
        to_w = (at_x, at_y)
        u_in, w_in = {}, {}

        def send_w(p, cu, k):
            u, w = pos[p]
            for o in (1, -1):
                r = blk(p, cu, w)
                w_in[p, k, o] = rcopy(r, r, to_w[p](o))

        def fwd_w(p, k):
            u, w = pos[p]
            cu = (u + k) % 4
            w_in[p, k, 1].wait_recv()
            r = blk(p, cu, (w + 3) % 4, 0)
            w_in[p, k, 2] = rcopy(r, r, to_w[p](1))
            w_in[p, k, -1].wait_recv()
            r = blk(p, cu, (w + 1) % 4, 1)
            w_in[p, k, -2] = rcopy(r, r, to_w[p](-1))

        for p in (0, 1):
            u, w = pos[p]
            r = blk(p, u, w)
            u_in[p, 1] = rcopy(r, r, to_u[p](1))
            u_in[p, -1] = rcopy(r, r, to_u[p](-1))
        for p in (0, 1):
            send_w(p, pos[p][0], 0)
        for p in (0, 1):
            u, w = pos[p]
            u_in[p, 1].wait_recv()
            r = blk(p, (u + 3) % 4, w, 0)
            u_in[p, 2] = rcopy(r, r, to_u[p](1))
            u_in[p, -1].wait_recv()
            r = blk(p, (u + 1) % 4, w, 1)
            u_in[p, -2] = rcopy(r, r, to_u[p](-1))
        for p in (0, 1):
            u, w = pos[p]
            send_w(p, (u + 3) % 4, 3)
            send_w(p, (u + 1) % 4, 1)
        for p in (0, 1):
            fwd_w(p, 0)
        for p in (0, 1):
            u, w = pos[p]
            u_in[p, 2].wait_recv()
            u_in[p, -2].wait_recv()
            send_w(p, (u + 2) % 4, 2)
        for k in (3, 1, 2):
            for p in (0, 1):
                fwd_w(p, k)
        for k in (0, 3, 1, 2):
            for p in (0, 1):
                w_in[p, k, 2].wait_recv()
                w_in[p, k, -2].wait_recv()

    gather_xy(xb)

    def norm_step(i, carry):
        run, b = i // 16, i % 16
        rows = pl.ds(pl.multiple_of(b * 16, 16), 16)
        values = xb[run, rows, :].astype(F32)
        inverse = lax.rsqrt(jnp.mean(values * values, axis=1, keepdims=True) + EPS)
        nb[run, rows, :] = (values * inverse * gain_ref[...]).astype(BF16)
        return carry

    lax.fori_loop(0, 32, norm_step, 0)

    wl[0].wait()
    wc[0].wait_recv()
    acc[...] = jnp.zeros_like(acc)
    id_c = meta_ref[:, 0:1]
    id_p = meta_ref[:, 1:2]
    active = meta_ref[:, 2:3].astype(F32)

    def target_of(j):
        base = ((z * 2 + j // 2) * 16 + f) * VL + (j % 2) * TN
        vocab = base + lax.broadcasted_iota(jnp.int32, (1, TN), 1)
        return (id_c == vocab).astype(F32) - (id_p == vocab).astype(F32)

    def fold(a):
        return a[:, :128] + a[:, 128:]

    def logit_step(j, carry):
        cols = pl.ds(pl.multiple_of((j % 2) * TN, TN), TN)
        raw = jnp.dot(
            nb[...].reshape(512, D), wv[j // 2, :, cols], preferred_element_type=F32
        )
        logit = CAP * jnp.tanh(raw / CAP)
        ex = jnp.exp(logit - CAP)
        lc, lp = logit[:256], logit[256:]
        ec, ep = ex[:256], ex[256:]
        lpb[j] = lp
        ecb[j] = ec
        epb[j] = ep
        acc[0] += fold(ec)
        acc[1] += fold(ep)
        acc[2] += fold(ec * (lc - lp))
        acc[3] += fold(target_of(j) * lp)
        return carry

    lax.fori_loop(0, 4, logit_step, 0)

    lane = lax.broadcasted_iota(jnp.int32, (256, 128), 1)
    stat = jnp.zeros((256, 128), F32)
    for s in range(4):
        stat = jnp.where(lane == s, jnp.sum(acc[s], axis=1, keepdims=True), stat)
    sx[x] = jnp.transpose(stat)[:8]
    sc = [rcopy(sx.at[x], sx.at[x], at_x(o)) for o in (2, 1, 3)]

    wl[1].wait()
    wc[1].wait_recv()
    wl[3].wait()
    wc[3].wait_recv()

    def enc_step(j, carry):
        cols = pl.ds(pl.multiple_of((j % 2) * TN, TN), TN)
        pre = jnp.dot(
            xb[...].reshape(512, D), ev[j // 2, :, cols], preferred_element_type=F32
        )
        bias = btv[j // 2, 0:1, cols]
        thr = btv[j // 2, 1:2, cols]
        a = jnp.maximum(pre + bias - thr, 0.0)
        difb[j] = a[256:] - a[:256]
        return carry

    lax.fori_loop(0, 2, enc_step, 0)
    for d in sc:
        d.wait_recv()
    sy[y] = sx[0] + sx[1] + sx[2] + sx[3]
    sc = [rcopy(sy.at[y], sy.at[y], at_y(o)) for o in (2, 1, 3)]
    lax.fori_loop(2, 3, enc_step, 0)
    for d in sc:
        d.wait_recv()
    sz[z] = sy[0] + sy[1] + sy[2] + sy[3]
    sc = [rcopy(sz.at[z], sz.at[z], at_z(o)) for o in (4, 3, 5, 2, 6, 1, 7)]
    lax.fori_loop(3, 4, enc_step, 0)
    for d in sc:
        d.wait_recv()
    tot = sz[0]
    for k in range(1, 8):
        tot = tot + sz[k]
    cols4 = jnp.transpose(jnp.concatenate([tot, jnp.zeros((120, 256), F32)], axis=0))
    total_c, total_p = cols4[:, 0:1], cols4[:, 1:2]
    cross, picked = cols4[:, 2:3], cols4[:, 3:4]
    per_token = active * (cross / total_c - jnp.log(total_c) + jnp.log(total_p) + picked)

    def pair_sum(a):
        return jnp.concatenate([a[2 * p : 2 * p + 1] + a[2 * p + 1 : 2 * p + 2] for p in range(8)], 0)

    met[c] = pair_sum(
        jnp.sum(jnp.broadcast_to(per_token, (256, 128)).reshape(16, 16, 128), axis=0)
    )
    mc = rcopy(met.at[c], met.at[c], sib)

    def dlogit_step(j, carry):
        slope = 1.0 - (lpb[j] / CAP) ** 2
        dl = active * (epb[j] / total_p - ecb[j] / total_c + target_of(j)) * slope
        dlb[j] = dl.astype(BF16)
        return carry

    lax.fori_loop(0, 4, dlogit_step, 0)

    def dnormed(q):
        rows = pl.ds(q * QUART, QUART)
        s = None
        for j in range(4):
            t = lax.dot_general(
                dlb[j],
                wv[j // 2, rows, (j % 2) * TN : (j % 2 + 1) * TN],
                NT,
                preferred_element_type=F32,
            )
            s = t if s is None else s + t
        pb[:, :, :, q * QUART : (q + 1) * QUART] = s.reshape(4, 4, 16, QUART).astype(BF16)

    pos = ((y, x), (x, y))
    to_u = (at_y, at_x)
    to_w = (at_x, at_y)

    def pcols(p, half):
        return pl.ds(p * PART + half * QUART, QUART)

    def chunk_w(p, cw, half):
        if p == 0:
            return pb.at[cw, :, :, pcols(p, half)]
        return pb.at[:, cw, :, pcols(p, half)]

    def chunk_u(p, cu, half):
        return qb.at[p, cu, :, pl.ds(half * QUART, QUART)]

    def rs_start(p, half, chunk, r1, r2, c_pos, to):
        o = 1 if half == 0 else -1
        a = rcopy(chunk(p, (c_pos + 2) % 4, half), r1.at[p, half], to(o))
        b = rcopy(chunk(p, (c_pos + 4 - o) % 4, half), r2.at[p, 1 - half, half], to(-o))
        return a, b

    def rs_mid(p, half, chunk, r1, r2, c_pos, to, a):
        o = 1 if half == 0 else -1
        a.wait_recv()
        ch = chunk(p, (c_pos + 4 + o) % 4, half)
        ch[...] = (ch[...].astype(F32) + r1[p, half].astype(F32)).astype(BF16)
        return rcopy(ch, r2.at[p, half, half], to(o))

    w1, w2 = {}, {}
    for q in range(4):
        p, half = q // 2, q % 2
        dnormed(q)
        w1[p, half] = rs_start(p, half, chunk_w, r1w, r2w, pos[p][1], to_w[p])
    for p in (0, 1):
        for half in (0, 1):
            w2[p, half] = rs_mid(p, half, chunk_w, r1w, r2w, pos[p][1], to_w[p], w1[p, half][0])
    u1, u2 = {}, {}
    for p in (0, 1):
        u, w = pos[p]
        for half in (0, 1):
            w1[p, half][1].wait_recv()
            w2[p, half].wait_recv()
            s = (
                chunk_w(p, w, half)[...].astype(F32)
                + r2w[p, 0, half].astype(F32)
                + r2w[p, 1, half].astype(F32)
            )
            qb[p, :, :, half * QUART : (half + 1) * QUART] = s.astype(BF16)
            u1[p, half] = rs_start(p, half, chunk_u, r1u, r2u, u, to_u[p])
    for p in (0, 1):
        for half in (0, 1):
            u2[p, half] = rs_mid(p, half, chunk_u, r1u, r2u, pos[p][0], to_u[p], u1[p, half][0])
    for p in (0, 1):
        u, w = pos[p]
        for half in (0, 1):
            u1[p, half][1].wait_recv()
            u2[p, half].wait_recv()
            s = (
                chunk_u(p, u, half)[...].astype(F32)
                + r2u[p, 0, half].astype(F32)
                + r2u[p, 1, half].astype(F32)
            )
            tb[:, :, pcols(p, half)] = s.reshape(2, 8, QUART).astype(BF16)

    def zcols(k):
        return pl.ds(pl.multiple_of((k % 4) * QUART, 128), QUART)

    zs = []
    for o in (4, 3, 5, 2, 6, 1, 7):
        k = (z + o) % 8
        zs.append(rcopy(tb.at[k // 4, :, zcols(k)], zr.at[z], at_z(o)))
    zr[z] = tb[z // 4, :, zcols(z)]
    for d in zs:
        d.wait_recv()
    s = zr[0].astype(F32)
    for k in range(1, 8):
        s = s + zr[k].astype(F32)
    vb[z // 4, :, zcols(z)] = s.astype(BF16)
    mine = vb.at[z // 4, :, zcols(z)]
    zs = [rcopy(mine, mine, at_z(o)) for o in (4, 3, 5, 2, 6, 1, 7)]
    for d in zs:
        d.wait_recv()

    values = xb[1, pl.ds(own, 16), :].astype(F32)
    inverse = lax.rsqrt(jnp.mean(values * values, axis=1, keepdims=True) + EPS)
    weighted = vb[...].astype(F32).reshape(16, D) * gain_ref[...]
    inner = jnp.sum(weighted * values, axis=1, keepdims=True)
    grad = inverse * weighted - inverse * inverse * inverse * values * inner / D
    gb[0, pl.ds(own, 16), :] = grad.astype(BF16)
    gather_xy(gb)

    wl[2].wait()
    wc[2].wait_recv()

    def proj_step(j, carry):
        rows = pl.ds(pl.multiple_of((j % 2) * TN, TN), TN)
        proj = lax.dot_general(
            gb[0], dv[j // 2, rows, :], NT, preferred_element_type=F32
        )
        a = jnp.sum((difb[j] * proj).reshape(16, 16, TN), axis=0)
        fin[j // 2, :, pl.ds(pl.multiple_of((j % 2) * TN, TN), TN)] = pair_sum(a)
        return carry

    lax.fori_loop(0, 4, proj_step, 0)
    fc = rcopy(fin.at[1 - c], finr, sib)
    fc.wait_recv()
    attr_ref[...] = fin[c] + finr[...]
    mc.wait_recv()
    metric_ref[...] = met[0] + met[1]
    for d in sent:
        d.wait_send()


def local(
    clean_hidden, patched_hidden, unembed, norm_gain, enc_weight, enc_bias, threshold,
    dec_weight, clean_next, patched_next, patch_pos,
):
    v = lax.axis_index("vocab")
    c = v % 2

    def mine(a):
        a = lax.dynamic_index_in_dim(a.reshape(8, 2, 4, 4, 2), c, 1, keepdims=False)
        return a.transpose(2, 1, 0, 3).reshape(256)

    token = jnp.arange(512, dtype=jnp.int32)
    active = (token.reshape(8, SEQ) % SEQ >= patch_pos[:, None]).astype(jnp.int32).reshape(512)
    meta = jnp.stack([mine(clean_next), mine(patched_next), mine(active)], axis=1)
    bt = jnp.stack([enc_bias, threshold], axis=0)
    any_spec = pl.BlockSpec(memory_space=pl.ANY)
    vm = pl.BlockSpec(memory_space=pltpu.VMEM)
    V = pltpu.VMEM
    scratch = [
        V((2, D, VL), BF16), V((2, D, VL), BF16), V((2, VL, D), BF16),
        V((8, 2, 2, D), BF16), V((2, 16, D), F32),
        V((2, 256, D), BF16), V((2, 256, D), BF16),
        V((4, 256, TN), F32), V((4, 256, TN), F32), V((4, 256, TN), F32),
        V((4, 256, TN), F32), V((4, 256, TN), BF16),
        V((4, 4, 16, D), BF16),
        V((2, 2, 4, 16, QUART), BF16), V((2, 2, 2, 4, 16, QUART), BF16),
        V((2, 4, 16, PART), BF16),
        V((2, 2, 16, QUART), BF16), V((2, 2, 2, 16, QUART), BF16),
        V((2, 8, D), BF16), V((8, 8, QUART), BF16), V((2, 8, D), BF16),
        V((1, 256, D), BF16),
        V((4, 8, 256), F32), V((4, 8, 256), F32), V((8, 8, 256), F32),
        V((4, 256, 128), F32),
        V((2, 8, VL), F32), V((8, VL), F32),
        V((2, 8, 128), F32), V((8, 128), F32),
        V((2, 2, VL), F32), V((2, VL), F32),
        pltpu.SemaphoreType.DMA((NCOPY,)), pltpu.SemaphoreType.DMA((NCOPY,)),
        pltpu.SemaphoreType.DMA((6,)),
    ]
    attr, met = pl.pallas_call(
        kernel,
        out_shape=(jax.ShapeDtypeStruct((8, VL), F32), jax.ShapeDtypeStruct((8, 128), F32)),
        in_specs=[any_spec] * 5 + [vm, any_spec, vm],
        out_specs=(vm, vm),
        scratch_shapes=scratch,
        compiler_params=pltpu.CompilerParams(
            collective_id=0, has_side_effects=True, vmem_limit_bytes=64_000_000
        ),
    )(
        clean_hidden, patched_hidden, unembed, enc_weight, dec_weight,
        norm_gain.reshape(1, D), bt, meta,
    )
    return attr, met[:, 0]


def solution(mesh):
    rows = P(("vocab", "feat"), None)
    cols = P(None, ("vocab", "feat"))
    vec = P(("vocab", "feat"))
    in_specs = (rows, rows, cols, P(), cols, vec, vec, rows, P(), P(), P())
    return jax.shard_map(
        local, mesh=mesh, in_specs=in_specs, out_specs=(cols, P()), check_vma=False
    )
```
